256 devices in a mesh: anim: 16 (over y, x_lo, core), snp: 16 (over z, x_hi).
Axes of the slice: x: 4 (x_hi: 2, x_lo: 2; x = x_hi * 2 + x_lo), y: 4, z: 8, core: 2. Of those that a mesh axis runs over, the one named last changes fastest.
Arguments:
- core_geno: bfloat16 [12288, 49152], P('anim', 'snp'), may hold values from -10 to 10, as said below
- noncore_geno: bfloat16 [12288, 49152], P('anim', 'snp'), may hold values from -10 to 10, as said below
- core_inv: bfloat16 [12288, 12288], P('anim', 'snp'), may hold values from -0.0546875 to 0.0546875
- snp_effects: bfloat16 [256, 49152], P(None, 'snp'), may hold values from -0.02734375 to 0.02734375
- noncore_scale: float32 [12288], P('anim'), may hold values from 0.5 to 2
Outputs:
- noncore_out: float32 [256, 12288], P(None, 'anim')
- core_out: float32 [256, 12288], P(None, ('anim', 'snp'))
The draws below stay inside these ranges and needn't reach their ends.
Inputs may be any that keep to these rules, and one draw needn't show every extreme that they name: `core_geno`: each column j is (c - 2 p_j) / sqrt(2 p_j (1 - p_j)) for codes c in 0, 1, 2 and a column frequency p_j shared with noncore_geno. `noncore_geno`: each column j is (c - 2 p_j) / sqrt(2 p_j (1 - p_j)) for codes c in 0, 1, 2 and a column frequency p_j shared with core_geno.
All inputs are finite; a program needn't handle non-finite values.
Results may differ from the reference program's by a relative error of at most 0.008.
Values may be sent and summed in bfloat16 or wider, within the bound.
A program may use at most 64 MiB of HBM per device.

```python
import math
import jax
import jax.numpy as jnp
from jax import lax

NSNP = 49152
NCORE = 12288
REPS = 256
NNON = 12288


def genotype_rows(key, count, salt):
    lowest = 0.05
    freq = jax.random.uniform(jax.random.fold_in(key, 11), (NSNP,), jnp.float32, lowest, 0.5)
    spread = jnp.sqrt(2.0 * freq * (1.0 - freq))
    row_key = jax.random.fold_in(key, salt)

    def one_row(index):
        draws = jax.random.uniform(jax.random.fold_in(row_key, index), (2, NSNP), jnp.float32)
        codes = jnp.sum((draws < freq[None, :]).astype(jnp.float32), axis=0)
        return ((codes - 2.0 * freq) / spread).astype(jnp.bfloat16)
    return lax.map(one_row, jnp.arange(count, dtype=jnp.int32))


def draw_core_geno(key, part):
    return genotype_rows(key, NCORE, 23)


def draw_noncore_geno(key, part):
    return genotype_rows(key, NNON, 37)


def level_of(stream_key, shape, cuts, low, largest):
    gain, own = 1.0, jax.random.fold_in(stream_key, 6)
    for axis_at, blocks in cuts:
        heights = jnp.exp(jax.random.uniform(jax.random.fold_in(own, axis_at), (blocks,), jnp.float32, low / len(cuts), largest / len(cuts)))
        gain = gain * jnp.repeat(heights, shape[axis_at] // blocks).reshape([-1 if axis == axis_at else 1 for axis in range(len(shape))])
    return gain


def centred(rng, dims, deviation, bound, split=(), kind=jnp.bfloat16):
    entries = jax.random.normal(rng, dims, jnp.float32) * deviation
    if len(split) > 0:
        entries = level_of(rng, dims, split, -0.22, 0.18) * entries
    return jnp.clip(entries, min=-bound, max=bound).astype(kind)


def setup_inputs(seed: int = 0) -> dict:
    key_of = jax.random.split(jax.random.key(seed), 6)
    core_geno = draw_core_geno(jax.random.fold_in(key_of[5], 71), 0)
    noncore_geno = draw_noncore_geno(jax.random.fold_in(key_of[5], 71), 0)
    core_inv = centred(key_of[2], (NCORE, NCORE), NCORE ** -0.5, 0.0546875, ((0, 16), (1, 16)))
    snp_effects = centred(key_of[3], (REPS, NSNP), NSNP ** -0.5, 0.02734375, ((1, 16),))
    noncore_scale = jnp.clip(jnp.exp(math.log(2.0) - 1.3862944 * jax.random.uniform(key_of[4], (NNON,), jnp.float32) ** level_of(key_of[4], (NNON,), ((0, 16),), -0.2, 0.2)), 0.5, 2.0)
    return dict(core_geno=core_geno, noncore_geno=noncore_geno, core_inv=core_inv, snp_effects=snp_effects, noncore_scale=noncore_scale)


def reference(core_geno, noncore_geno, core_inv, snp_effects, noncore_scale):
    f32 = jnp.float32
    bf16 = jnp.bfloat16
    core_vals = jnp.dot(snp_effects, core_geno.T, preferred_element_type=f32).astype(bf16)
    noncore_vals = jnp.dot(snp_effects, noncore_geno.T, preferred_element_type=f32)
    core_weights = jnp.dot(core_vals, core_inv.T, preferred_element_type=f32).astype(bf16)
    snp_core = (jnp.dot(core_weights, core_geno, preferred_element_type=f32) / NSNP).astype(bf16)
    predicted = jnp.dot(snp_core, noncore_geno.T, preferred_element_type=f32)
    noncore_out = noncore_scale[None, :] * (noncore_vals - predicted)
    noncore_half = noncore_out.astype(bf16)
    snp_noncore = (jnp.dot(noncore_half, noncore_geno, preferred_element_type=f32) / NSNP).astype(bf16)
    back = jnp.dot(snp_noncore, core_geno.T, preferred_element_type=f32)
    core_rest = (core_vals.astype(f32) - back).astype(bf16)
    core_out = jnp.dot(core_rest, core_inv.T, preferred_element_type=f32)
    return noncore_out, core_out
```

```python
import functools

import jax
import jax.numpy as jnp
from jax import lax
from jax.experimental import pallas as pl
from jax.experimental.pallas import tpu as pltpu
from jax.sharding import PartitionSpec as P

NSNP = 49152
MESH = pl.DeviceIdType.MESH
BATCHES = 2
COL_SPLIT = 2
LAG = 3

f32 = jnp.float32
bf16 = jnp.bfloat16


def nt_dot(left, right):
    return lax.dot_general(
        left, right, (((1,), (1,)), ((), ())), preferred_element_type=f32
    )


def kernel(dims, core_hbm, noncore_hbm, inv_hbm, effects_hbm, scale_hbm,
           noncore_hbm_out, out_ref, *scratch):
    A, S, R, NA, NS, NI = dims
    NB, KC = BATCHES, COL_SPLIT
    Rb = R // NB
    KR = S // KC
    RC, W = Rb // KR, NA // KC
    chips = A // 2
    RA, H = Rb // chips, NS // 2
    OC = NA // S
    TN = min(256, NA)
    TE = min(512, H)
    (core, noncore, inv, effects, scale,
     pa, np_, ra, cv, tb, vc,
     pd, rd, wc, wf,
     xe, xr, ye, yb, re_, ze, me,
     pf, rf, nc, nf,
     xg, xh, yg, yc, rg, zg, mg,
     ph, rh, cr, tr, vr,
     op, ri,
     insem, outsem, send, recv, agsem) = scratch
    a = lax.axis_index("anim")
    s = lax.axis_index("snp")
    chip = a // 2
    half = a % 2
    partner = a + 1 - 2 * half

    loads = [(effects_hbm, effects), (core_hbm, core), (noncore_hbm, noncore),
             (inv_hbm, inv), (scale_hbm, scale)]
    copies = [pltpu.make_async_copy(x, y, insem.at[i]) for i, (x, y) in enumerate(loads)]
    for c in copies:
        c.start()

    barrier = pltpu.get_barrier_semaphore()

    def greet_snp(r, _):
        pl.semaphore_signal(barrier, inc=1, device_id={"snp": (s + r) % S}, device_id_type=MESH)
        return 0

    def greet_anim(r, _):
        pl.semaphore_signal(barrier, inc=1, device_id={"anim": (a + r) % A}, device_id_type=MESH)
        return 0

    lax.fori_loop(1, S, greet_snp, 0)
    lax.fori_loop(1, A, greet_anim, 0)

    @pl.when(a != s)
    def _():
        pl.semaphore_signal(barrier, inc=1, device_id={"anim": s, "snp": a}, device_id_type=MESH)
        pl.semaphore_wait(barrier, S + A - 1)

    @pl.when(a == s)
    def _():
        pl.semaphore_wait(barrier, S + A - 2)

    def rows(k):
        return pl.ds(pl.multiple_of((k % KR) * RC, RC), RC)

    def cols(k):
        return pl.ds(pl.multiple_of((k // KR) * W, W), W)

    def wait_bytes(ref, sem):
        pltpu.make_async_copy(ref, ref, sem).wait()

    ends = []

    def rs_snp(b, phase, part, got):
        def step(r, _):
            k = (s + r) % S
            pltpu.make_async_remote_copy(
                part.at[b, rows(k), cols(k)], got.at[b, r - 1],
                send.at[b, phase], recv.at[b, phase],
                device_id={"snp": k}, device_id_type=MESH).start()
            return 0
        lax.fori_loop(1, S, step, 0)
        ends.append((got.at[b], b, phase))

    def sum_snp(b, phase, part, got):
        wait_bytes(got.at[b], recv.at[b, phase])
        total = part[b, rows(s), cols(s)].astype(f32)
        for r in range(S - 1):
            total = total + got[b, r].astype(f32)
        return total

    def ag_snp(b, phase, chunk, whole, proxy):
        def step(r, _):
            pltpu.make_async_remote_copy(
                chunk.at[b], whole.at[b, rows(s), cols(s)],
                send.at[b, phase], recv.at[b, phase],
                device_id={"snp": (s + r) % S}, device_id_type=MESH).start()
            return 0
        lax.fori_loop(1, S, step, 0)
        whole[b, rows(s), cols(s)] = chunk[b]
        ends.append((proxy.at[b], b, phase))

    def turn(b, phase, chunk, landed):
        @pl.when(a != s)
        def _():
            pltpu.make_async_remote_copy(
                chunk.at[b], landed.at[b], send.at[b, phase], recv.at[b, phase],
                device_id={"anim": s, "snp": a}, device_id_type=MESH).start()

        @pl.when(a == s)
        def _():
            pltpu.make_async_copy(chunk.at[b], landed.at[b], recv.at[b, phase]).start()
        ends.append((None, b, phase))

    def ag_anim(b, turned, phase, landed, whole, proxy):
        wait_bytes(landed.at[b], recv.at[b, turned])

        def step(r, _):
            pltpu.make_async_remote_copy(
                landed.at[b], whole.at[b, rows(a), cols(a)],
                send.at[b, phase], recv.at[b, phase],
                device_id={"anim": (a + r) % A}, device_id_type=MESH).start()
            return 0
        lax.fori_loop(1, A, step, 0)
        whole[b, rows(a), cols(a)] = landed[b]
        ends.append((proxy.at[b], b, phase))

    def marker_product(b, phase, left, geno, out_half, in_half, own):
        lhs = left[b]

        def other(t, _):
            at = pl.ds(pl.multiple_of((1 - half) * H + t * TE, TE), TE)
            to = pl.ds(pl.multiple_of(t * TE, TE), TE)
            out_half[b, :, to] = jnp.dot(lhs, geno[:, at], preferred_element_type=f32).astype(bf16)
            pltpu.make_async_remote_copy(
                out_half.at[b, :, to], in_half.at[b, :, to],
                send.at[b, phase], recv.at[b, phase],
                device_id={"anim": partner}, device_id_type=MESH).start()
            return 0
        lax.fori_loop(0, H // TE, other, 0)

        def mine(t, _):
            at = pl.ds(pl.multiple_of(half * H + t * TE, TE), TE)
            to = pl.ds(pl.multiple_of(t * TE, TE), TE)
            own[b, :, to] = jnp.dot(lhs, geno[:, at], preferred_element_type=f32)
            return 0
        lax.fori_loop(0, H // TE, mine, 0)
        ends.append((in_half.at[b], b, phase))

    def chip_rows(c):
        return pl.ds(pl.multiple_of(c * RA, RA), RA)

    def rs_chips(b, crossed, phase, in_half, own, both, got):
        wait_bytes(in_half.at[b], recv.at[b, crossed])

        def step(r, _):
            c = (chip + r) % chips
            at = chip_rows(c)
            both[b, at, :] = (own[b, at, :] + in_half[b, at, :].astype(f32)).astype(bf16)
            pltpu.make_async_remote_copy(
                both.at[b, at, :], got.at[b, r - 1],
                send.at[b, phase], recv.at[b, phase],
                device_id={"anim": 2 * c + half}, device_id_type=MESH).start()
            return 0
        lax.fori_loop(1, chips, step, 0)
        ends.append((got.at[b], b, phase))

    def half_cols(h):
        return pl.ds(pl.multiple_of(h * H, H), H)

    def ag_chips(b, summed, phase, cross, slot, in_half, own, got, chunk, whole):
        at = chip_rows(chip)
        total = own[b, at, :] + in_half[b, at, :].astype(f32)
        wait_bytes(got.at[b], recv.at[b, summed])
        for r in range(chips - 1):
            total = total + got[b, r].astype(f32)
        chunk[b] = (total / NSNP).astype(bf16)
        spot = whole.at[b, at, half_cols(half)]

        def step(r, _):
            pltpu.make_async_remote_copy(
                chunk.at[b], spot, send.at[b, phase], agsem.at[b, slot, r - 1],
                device_id={"anim": 2 * ((chip + r) % chips) + half}, device_id_type=MESH).start()
            return 0
        lax.fori_loop(1, chips, step, 0)
        pltpu.make_async_remote_copy(
            chunk.at[b], spot, send.at[b, cross], recv.at[b, cross],
            device_id={"anim": partner}, device_id_type=MESH).start()
        whole[b, at, half_cols(half)] = chunk[b]
        ends.append((got.at[b], b, phase))
        ends.append((in_half.at[b], b, cross))

    def relay(b, cross, slot, whole):
        def step(r, _):
            c = (chip + chips - r) % chips
            spot = whole.at[b, chip_rows(c), half_cols(half)]
            wait_bytes(spot, agsem.at[b, slot, r - 1])
            pltpu.make_async_remote_copy(
                spot, spot, send.at[b, cross], recv.at[b, cross],
                device_id={"anim": partner}, device_id_type=MESH).start()
            return 0
        lax.fori_loop(1, chips, step, 0)

    def rep_rows(b):
        return pl.ds(b * Rb, Rb)

    def tiles(body):
        def step(t, _):
            body(pl.ds(pl.multiple_of(t * TN, TN), TN))
            return 0
        lax.fori_loop(0, NA // TN, step, 0)

    def s0(b):
        if b == 0:
            copies[0].wait()
            copies[1].wait()

        def body(at):
            pa[b, :, at] = nt_dot(effects[rep_rows(b), :], core[at, :]).astype(bf16)
        tiles(body)
        rs_snp(b, 0, pa, ra)

    def s0b(b):
        if b == 0:
            copies[2].wait()

        def body(at):
            np_[b, :, at] = nt_dot(effects[rep_rows(b), :], noncore[at, :])
        tiles(body)

    def s1(b):
        cv[b] = sum_snp(b, 0, pa, ra).astype(bf16)
        turn(b, 1, cv, tb)

    def s2(b):
        ag_anim(b, 1, 2, tb, vc, ra)

    def s3(b):
        if b == 0:
            copies[3].wait()
        wait_bytes(ra.at[b], recv.at[b, 2])

        def body(at):
            pd[b, :, at] = nt_dot(vc[b], inv[at, :]).astype(bf16)
        tiles(body)
        rs_snp(b, 3, pd, rd)

    def s4(b):
        wc[b] = sum_snp(b, 3, pd, rd).astype(bf16)
        ag_snp(b, 4, wc, wf, rd)

    def s5(b):
        wait_bytes(rd.at[b], recv.at[b, 4])
        marker_product(b, 5, wf, core, xe, xr, ye)

    def s6(b):
        rs_chips(b, 5, 6, xr, ye, yb, re_)

    def s7(b):
        ag_chips(b, 6, 7, 8, 0, xr, ye, re_, ze, me)

    def s8(b):
        relay(b, 8, 0, me)

    def s9(b):
        wait_bytes(xr.at[b], recv.at[b, 8])

        def body(at):
            pf[b, :, at] = (np_[b, :, at] - nt_dot(me[b], noncore[at, :])).astype(bf16)
        tiles(body)
        rs_snp(b, 9, pf, rf)

    def s10(b):
        if b == 0:
            copies[4].wait()
        nc[b] = (scale[:, cols(s)] * sum_snp(b, 9, pf, rf)).astype(bf16)
        ag_snp(b, 10, nc, nf, rf)

    def s11(b):
        wait_bytes(rf.at[b], recv.at[b, 10])
        pltpu.make_async_copy(nf.at[b], noncore_hbm_out.at[rep_rows(b), :], outsem.at[b]).start()
        marker_product(b, 11, nf, noncore, xg, xh, yg)

    def s12(b):
        rs_chips(b, 11, 12, xh, yg, yc, rg)

    def s13(b):
        ag_chips(b, 12, 13, 14, 1, xh, yg, rg, zg, mg)

    def s14(b):
        relay(b, 14, 1, mg)

    def s15(b):
        wait_bytes(xh.at[b], recv.at[b, 14])

        def body(at):
            ph[b, :, at] = nt_dot(mg[b], core[at, :]).astype(bf16)
        tiles(body)
        rs_snp(b, 15, ph, rh)

    def s16(b):
        cr[b] = (cv[b].astype(f32) - sum_snp(b, 15, ph, rh)).astype(bf16)
        turn(b, 16, cr, tr)

    def s17(b):
        ag_anim(b, 16, 17, tr, vr, rh)

    def s18(b):
        wait_bytes(rh.at[b], recv.at[b, 17])

        def body(at):
            op[b, at, :] = nt_dot(inv[at, :], vr[b]).astype(bf16)
        tiles(body)

        def step(r, _):
            k = (s + r) % S
            pltpu.make_async_remote_copy(
                op.at[b, pl.ds(pl.multiple_of(k * OC, OC), OC), :], ri.at[b, r - 1],
                send.at[b, 18], recv.at[b, 18],
                device_id={"snp": k}, device_id_type=MESH).start()
            return 0
        lax.fori_loop(1, S, step, 0)
        ends.append((ri.at[b], b, 18))

    def s19(b):
        wait_bytes(ri.at[b], recv.at[b, 18])
        total = op[b, pl.ds(pl.multiple_of(s * OC, OC), OC), :].astype(f32)
        for r in range(S - 1):
            total = total + ri[b, r].astype(f32)
        out_ref[:, b * Rb:(b + 1) * Rb] = total

    stages = [s0, s0b, s1, s2, s3, s4, s5, s6, s7, s8, s9, s10, s11, s12, s13,
              s14, s15, s16, s17, s18, s19]
    order = sorted((i + LAG * b, b, i) for i in range(len(stages)) for b in range(NB))
    for _, b, i in order:
        stages[i](b)

    for ref, b, phase in ends:
        if ref is None:
            @pl.when(a != s)
            def _():
                wait_bytes(tb.at[b], send.at[b, phase])
        else:
            wait_bytes(ref, send.at[b, phase])
    for b in range(NB):
        wait_bytes(nf.at[b], outsem.at[b])


def solution(mesh):
    A, S = mesh.shape["anim"], mesh.shape["snp"]

    def local(core_geno, noncore_geno, core_inv, snp_effects, noncore_scale):
        R = snp_effects.shape[0]
        NA, NS = core_geno.shape
        NI = core_inv.shape[1]
        NB, KC = BATCHES, COL_SPLIT
        Rb = R // NB
        KR = S // KC
        RC, W = Rb // KR, NA // KC
        chips = A // 2
        RA, H = Rb // chips, NS // 2
        OC = NA // S
        V = pltpu.VMEM
        chunk = V((NB, RC, W), bf16)
        part = V((NB, Rb, NA), bf16)
        got = V((NB, S - 1, RC, W), bf16)
        halfb = V((NB, Rb, H), bf16)
        marker = [halfb, halfb, V((NB, Rb, H), f32), halfb,
                  V((NB, chips - 1, RA, H), bf16), V((NB, RA, H), bf16), V((NB, Rb, NS), bf16)]
        scratch = [
            V((NA, NS), bf16), V((NA, NS), bf16), V((NA, NI), bf16), V((R, NS), bf16), V((1, NA), f32),
            part, V((NB, Rb, NA), f32), got, chunk, chunk, part,
            part, got, chunk, part,
            *marker,
            part, got, chunk, part,
            *marker,
            part, got, chunk, chunk, part,
            V((NB, NA, Rb), bf16), V((NB, S - 1, OC, Rb), bf16),
            pltpu.SemaphoreType.DMA((5,)), pltpu.SemaphoreType.DMA((NB,)),
            pltpu.SemaphoreType.DMA((NB, 19)), pltpu.SemaphoreType.DMA((NB, 19)),
            pltpu.SemaphoreType.DMA((NB, 2, chips - 1)),
        ]
        half_out, turned = pl.pallas_call(
            functools.partial(kernel, (A, S, R, NA, NS, NI)),
            out_shape=(jax.ShapeDtypeStruct((R, NA), bf16), jax.ShapeDtypeStruct((OC, R), f32)),
            in_specs=[pl.BlockSpec(memory_space=pl.ANY)] * 5,
            out_specs=(pl.BlockSpec(memory_space=pl.ANY), pl.BlockSpec(memory_space=pltpu.VMEM)),
            scratch_shapes=scratch,
            compiler_params=pltpu.CompilerParams(
                collective_id=0, has_side_effects=True, vmem_limit_bytes=60 * 1024 * 1024),
        )(core_geno, noncore_geno, core_inv, snp_effects, noncore_scale.reshape(1, -1))
        return half_out.astype(f32), turned.T

    return jax.shard_map(
        local,
        mesh=mesh,
        in_specs=(P("anim", "snp"), P("anim", "snp"), P("anim", "snp"), P(None, "snp"), P("anim")),
        out_specs=(P(None, "anim"), P(None, ("anim", "snp"))),
        check_vma=False,
    )
```

```python
import functools

import jax
import jax.numpy as jnp
from jax import lax
from jax.experimental import pallas as pl
from jax.experimental.pallas import tpu as pltpu
from jax.sharding import PartitionSpec as P

NSNP = 49152
MESH = pl.DeviceIdType.MESH
BATCHES = 2
COL_SPLIT = 2
LAG = 1

f32 = jnp.float32
bf16 = jnp.bfloat16


def nt_dot(left, right):
    return lax.dot_general(
        left, right, (((1,), (1,)), ((), ())), preferred_element_type=f32
    )


def kernel(dims, core_hbm, noncore_hbm, inv_hbm, effects_hbm, scale_hbm,
           noncore_hbm_out, out_ref, *scratch):
    A, S, R, NA, NS, NI = dims
    NB, KC = BATCHES, COL_SPLIT
    Rb = R // NB
    KR = S // KC
    RC, W = Rb // KR, NA // KC
    chips = A // 2
    RA, H = Rb // chips, NS // 2
    OC = NA // S
    TN = min(256, W)
    TE = min(512, H)
    (core, noncore, inv, effects, scale,
     pa, np_, ra, cv, tb, vc,
     pd, rd, wc, wf,
     xe, xr, ye, yb, re_, ze, me,
     pf, rf, nc, nf,
     xg, xh, yg, yc, rg, zg, mg,
     ph, rh, cr, tr, vr,
     op, ri,
     insem, outsem, send, recv, agsem) = scratch
    a = lax.axis_index("anim")
    s = lax.axis_index("snp")
    chip = a // 2
    half = a % 2
    partner = a + 1 - 2 * half

    fold = S // 4
    away = (s // 2 + S // 2 - a // 2) % (S // 2)
    near = away // fold
    drop = near * (away - fold) + (1 - near) * (fold - 1 - away)
    turn_row = (((a // 4 + drop) % (A // 4)) * 2 + ((a // 2) % 2 + s % 2 + a % 2) % 2) * 2 + 1 - near
    rise = (a // 4 + A // 4 - s // 4) % (A // 4)
    reach = half * (fold - 1 - rise) + (1 - half) * (fold + rise)
    index = ((s // 2 + reach) % (S // 2)) * 2 + (s % 2 + (a // 2) % 2 + (s // 2) % 2) % 2

    loads = [(effects_hbm, effects), (core_hbm, core), (noncore_hbm, noncore),
             (inv_hbm, inv), (scale_hbm, scale)]
    copies = [pltpu.make_async_copy(x, y, insem.at[i]) for i, (x, y) in enumerate(loads)]
    for c in copies:
        c.start()

    barrier = pltpu.get_barrier_semaphore()

    def greet_snp(r, _):
        pl.semaphore_signal(barrier, inc=1, device_id={"snp": (s + r) % S}, device_id_type=MESH)
        return 0

    def greet_anim(r, _):
        pl.semaphore_signal(barrier, inc=1, device_id={"anim": (a + r) % A}, device_id_type=MESH)
        return 0

    lax.fori_loop(1, S, greet_snp, 0)
    lax.fori_loop(1, A, greet_anim, 0)

    pl.semaphore_signal(barrier, inc=1, device_id={"anim": s, "snp": index}, device_id_type=MESH)

    def meet():
        pl.semaphore_wait(barrier, S + A - 1)

    def ring_step(j, n):
        return ((n - j) // 2) * (2 * (j % 2) - 1) % n

    rings, circles = S // 2, chips // 2
    snp_z, snp_x = s // 2, s % 2
    anim_y, anim_x = chip // 2, chip % 2
    flip = 1 - snp_x, snp_x
    side = 1 - anim_x, anim_x
    snp_peers = [lax.rem(snp_z + ring_step(i // 2, rings), rings) * 2 + flip[i % 2] for i in range(S - 1)]
    chip_peers = [lax.rem(anim_y + ring_step(i // 2, circles), circles) * 2 + side[i % 2] for i in range(chips - 1)]
    chip_backs = [lax.rem(anim_y + circles - ring_step(i // 2, circles), circles) * 2 + side[i % 2] for i in range(chips - 1)]
    anim_peers = [
        (lax.rem(anim_y + ring_step(i // 4, circles), circles) * 2 + side[i % 4 // 2]) * 2
        + (1 - half if i % 2 == 0 else half) for i in range(A - 1)]

    def rows(k):
        return pl.ds(pl.multiple_of((k // KC) * RC, RC), RC)

    def cols(k):
        return pl.ds(pl.multiple_of((k % KC) * W, W), W)

    def wait_bytes(ref, sem):
        pltpu.make_async_copy(ref, ref, sem).wait()

    ends = []

    def send_part(b, phase, part, got, which):
        for r in which:
            k = snp_peers[r]
            pltpu.make_async_remote_copy(
                part.at[b, rows(k), cols(k)], got.at[b, r],
                send.at[b, phase], recv.at[b, phase],
                device_id={"snp": k}, device_id_type=MESH).start()

    def rs_snp(b, phase, part, got):
        send_part(b, phase, part, got, range(S - 1))
        ends.append((got.at[b], b, phase))

    def tiles_rs_snp(b, phase, part, got, body):
        count = NA // TN
        early = -(-W // TN)

        def step(t, _):
            at = snp_x * t + (1 - snp_x) * (count - 1 - t)
            body(pl.ds(pl.multiple_of(at * TN, TN), TN))
            return 0
        lax.fori_loop(0, early, step, 0)
        send_part(b, phase, part, got, range(0, S - 1, 2))
        lax.fori_loop(early, count, step, 0)
        send_part(b, phase, part, got, range(1, S - 1, 2))
        ends.append((got.at[b], b, phase))

    def sum_snp(b, phase, part, got):
        wait_bytes(got.at[b], recv.at[b, phase])
        total = part[b, rows(s), cols(s)].astype(f32)
        for r in range(S - 1):
            total = total + got[b, r].astype(f32)
        return total

    def ag_snp(b, phase, chunk, whole, proxy):
        for r in range(S - 1):
            pltpu.make_async_remote_copy(
                chunk.at[b], whole.at[b, rows(s), cols(s)],
                send.at[b, phase], recv.at[b, phase],
                device_id={"snp": snp_peers[r]}, device_id_type=MESH).start()
        whole[b, rows(s), cols(s)] = chunk[b]
        ends.append((proxy.at[b], b, phase))

    def turn(b, phase, chunk, landed):
        pltpu.make_async_remote_copy(
            chunk.at[b], landed.at[b], send.at[b, phase], recv.at[b, phase],
            device_id={"anim": turn_row, "snp": a}, device_id_type=MESH).start()
        ends.append((landed.at[b], b, phase))

    def ag_anim(b, turned, phase, landed, whole, proxy):
        wait_bytes(landed.at[b], recv.at[b, turned])

        for r in range(A - 1):
            pltpu.make_async_remote_copy(
                landed.at[b], whole.at[b, rows(index), cols(index)],
                send.at[b, phase], recv.at[b, phase],
                device_id={"anim": anim_peers[r]}, device_id_type=MESH).start()
        whole[b, rows(index), cols(index)] = landed[b]
        ends.append((proxy.at[b], b, phase))

    def marker_product(b, phase, left, geno, out_half, in_half, own):
        lhs = left[b]

        def other(t, _):
            at = pl.ds(pl.multiple_of((1 - half) * H + t * TE, TE), TE)
            to = pl.ds(pl.multiple_of(t * TE, TE), TE)
            out_half[b, :, to] = jnp.dot(lhs, geno[:, at], preferred_element_type=f32).astype(bf16)
            pltpu.make_async_remote_copy(
                out_half.at[b, :, to], in_half.at[b, :, to],
                send.at[b, phase], recv.at[b, phase],
                device_id={"anim": partner}, device_id_type=MESH).start()
            return 0
        lax.fori_loop(0, H // TE, other, 0)

        def mine(t, _):
            at = pl.ds(pl.multiple_of(half * H + t * TE, TE), TE)
            to = pl.ds(pl.multiple_of(t * TE, TE), TE)
            own[b, :, to] = jnp.dot(lhs, geno[:, at], preferred_element_type=f32)
            return 0
        lax.fori_loop(0, H // TE, mine, 0)
        ends.append((in_half.at[b], b, phase))

    def chip_rows(c):
        return pl.ds(pl.multiple_of(c * RA, RA), RA)

    def rs_chips(b, crossed, phase, in_half, own, both, got):
        wait_bytes(in_half.at[b], recv.at[b, crossed])

        for r in range(chips - 1):
            c = chip_peers[r]
            at = chip_rows(c)
            both[b, at, :] = (own[b, at, :] + in_half[b, at, :].astype(f32)).astype(bf16)
            pltpu.make_async_remote_copy(
                both.at[b, at, :], got.at[b, r],
                send.at[b, phase], recv.at[b, phase],
                device_id={"anim": 2 * c + half}, device_id_type=MESH).start()
        ends.append((got.at[b], b, phase))

    def half_cols(h):
        return pl.ds(pl.multiple_of(h * H, H), H)

    def ag_chips(b, summed, phase, cross, slot, in_half, own, got, chunk, whole):
        at = chip_rows(chip)
        total = own[b, at, :] + in_half[b, at, :].astype(f32)
        wait_bytes(got.at[b], recv.at[b, summed])
        for r in range(chips - 1):
            total = total + got[b, r].astype(f32)
        chunk[b] = (total / NSNP).astype(bf16)
        spot = whole.at[b, at, half_cols(half)]

        for r in range(chips - 1):
            pltpu.make_async_remote_copy(
                chunk.at[b], spot, send.at[b, phase], agsem.at[b, slot, r],
                device_id={"anim": 2 * chip_peers[r] + half}, device_id_type=MESH).start()
        pltpu.make_async_remote_copy(
            chunk.at[b], spot, send.at[b, cross], recv.at[b, cross],
            device_id={"anim": partner}, device_id_type=MESH).start()
        whole[b, at, half_cols(half)] = chunk[b]
        ends.append((got.at[b], b, phase))
        ends.append((in_half.at[b], b, cross))

    def relay(b, cross, slot, whole):
        for r in range(chips - 1):
            spot = whole.at[b, chip_rows(chip_backs[r]), half_cols(half)]
            wait_bytes(spot, agsem.at[b, slot, r])
            pltpu.make_async_remote_copy(
                spot, spot, send.at[b, cross], recv.at[b, cross],
                device_id={"anim": partner}, device_id_type=MESH).start()

    def rep_rows(b):
        return pl.ds(b * Rb, Rb)

    def tiles(body):
        def step(t, _):
            body(pl.ds(pl.multiple_of(t * TN, TN), TN))
            return 0
        lax.fori_loop(0, NA // TN, step, 0)

    def s0(b):
        if b == 0:
            copies[0].wait()
            copies[1].wait()

        def body(at):
            pa[b, :, at] = nt_dot(effects[rep_rows(b), :], core[at, :]).astype(bf16)
        tiles(body)

    def s0a(b):
        if b == 0:
            meet()
        rs_snp(b, 0, pa, ra)

    def s0b(b):
        if b == 0:
            copies[2].wait()

        def body(at):
            np_[b, :, at] = nt_dot(effects[rep_rows(b), :], noncore[at, :])
        tiles(body)

    def s1(b):
        cv[b] = sum_snp(b, 0, pa, ra).astype(bf16)
        turn(b, 1, cv, tb)

    def s2(b):
        ag_anim(b, 1, 2, tb, vc, ra)

    def s3(b):
        if b == 0:
            copies[3].wait()
        wait_bytes(ra.at[b], recv.at[b, 2])

        def body(at):
            pd[b, :, at] = nt_dot(vc[b], inv[at, :]).astype(bf16)
        tiles_rs_snp(b, 3, pd, rd, body)

    def s4(b):
        wc[b] = sum_snp(b, 3, pd, rd).astype(bf16)
        ag_snp(b, 4, wc, wf, rd)

    def s5(b):
        wait_bytes(rd.at[b], recv.at[b, 4])
        marker_product(b, 5, wf, core, xe, xr, ye)

    def s6(b):
        rs_chips(b, 5, 6, xr, ye, yb, re_)

    def s7(b):
        ag_chips(b, 6, 7, 8, 0, xr, ye, re_, ze, me)

    def s8(b):
        relay(b, 8, 0, me)

        def body(at):
            np_[b, :, at] = np_[b, :, at] - nt_dot(me[b, :, half_cols(half)], noncore[at, half_cols(half)])
        tiles(body)

    def s9(b):
        wait_bytes(xr.at[b], recv.at[b, 8])

        def body(at):
            pf[b, :, at] = (np_[b, :, at] - nt_dot(
                me[b, :, half_cols(1 - half)], noncore[at, half_cols(1 - half)])).astype(bf16)
        tiles_rs_snp(b, 9, pf, rf, body)

    def s10(b):
        if b == 0:
            copies[4].wait()
        first = (s % KC) * (W // 128)
        line = jnp.concatenate([scale[pl.ds(first + q, 1), :] for q in range(W // 128)], axis=1)
        nc[b] = (line * sum_snp(b, 9, pf, rf)).astype(bf16)
        ag_snp(b, 10, nc, nf, rf)

    def s11(b):
        wait_bytes(rf.at[b], recv.at[b, 10])
        pltpu.make_async_copy(nf.at[b], noncore_hbm_out.at[rep_rows(b), :], outsem.at[b]).start()
        marker_product(b, 11, nf, noncore, xg, xh, yg)

    def s12(b):
        rs_chips(b, 11, 12, xh, yg, yc, rg)

    def s13(b):
        ag_chips(b, 12, 13, 14, 1, xh, yg, rg, zg, mg)

    def s14(b):
        relay(b, 14, 1, mg)

        def body(at):
            np_[b, :, at] = nt_dot(mg[b, :, half_cols(half)], core[at, half_cols(half)])
        tiles(body)

    def s15(b):
        wait_bytes(xh.at[b], recv.at[b, 14])

        def body(at):
            ph[b, :, at] = (np_[b, :, at] + nt_dot(
                mg[b, :, half_cols(1 - half)], core[at, half_cols(1 - half)])).astype(bf16)
        tiles_rs_snp(b, 15, ph, rh, body)

    def s16(b):
        cr[b] = (cv[b].astype(f32) - sum_snp(b, 15, ph, rh)).astype(bf16)
        turn(b, 16, cr, tr)

    def s17(b):
        ag_anim(b, 16, 17, tr, vr, rh)

    def s18(b):
        wait_bytes(rh.at[b], recv.at[b, 17])

        op[b] = nt_dot(inv[...], vr[b]).astype(bf16)

        for r in range(S - 1):
            k = snp_peers[r]
            pltpu.make_async_remote_copy(
                op.at[b, pl.ds(pl.multiple_of(k * OC, OC), OC), :], ri.at[b, r],
                send.at[b, 18], recv.at[b, 18],
                device_id={"snp": k}, device_id_type=MESH).start()
        ends.append((ri.at[b], b, 18))

    def s19(b):
        wait_bytes(ri.at[b], recv.at[b, 18])
        total = op[b, pl.ds(pl.multiple_of(s * OC, OC), OC), :].astype(f32)
        for r in range(S - 1):
            total = total + ri[b, r].astype(f32)
        out_ref[:, b * Rb:(b + 1) * Rb] = total

    stages = [s0, s0a, s0b, s1, s2, s3, s4, s5, s6, s7, s8, s9, s10, s11, s12, s13,
              s14, s15, s16, s17, s18, s19]
    order = sorted((i + LAG * b, b, i) for i in range(len(stages)) for b in range(NB))
    for _, b, i in order:
        stages[i](b)

    for ref, b, phase in ends:
        wait_bytes(ref, send.at[b, phase])
    for b in range(NB):
        wait_bytes(nf.at[b], outsem.at[b])


def widen(half_ref, turned_ref, noncore_ref, core_ref):
    noncore_ref[...] = half_ref[...].astype(f32)
    core_ref[...] = turned_ref[...]


def solution(mesh):
    A, S = mesh.shape["anim"], mesh.shape["snp"]

    def local(core_geno, noncore_geno, core_inv, snp_effects, noncore_scale):
        R = snp_effects.shape[0]
        NA, NS = core_geno.shape
        NI = core_inv.shape[1]
        NB, KC = BATCHES, COL_SPLIT
        Rb = R // NB
        KR = S // KC
        RC, W = Rb // KR, NA // KC
        chips = A // 2
        RA, H = Rb // chips, NS // 2
        OC = NA // S
        V = pltpu.VMEM
        chunk = V((NB, RC, W), bf16)
        part = V((NB, Rb, NA), bf16)
        got = V((NB, S - 1, RC, W), bf16)
        halfb = V((NB, Rb, H), bf16)
        marker = [halfb, halfb, V((NB, Rb, H), f32), halfb,
                  V((NB, chips - 1, RA, H), bf16), V((NB, RA, H), bf16), V((NB, Rb, NS), bf16)]
        scratch = [
            V((NA, NS), bf16), V((NA, NS), bf16), V((NA, NI), bf16), V((R, NS), bf16), V((NA // 128, 128), f32),
            part, V((NB, Rb, NA), f32), got, chunk, chunk, part,
            part, got, chunk, part,
            *marker,
            part, got, chunk, part,
            *marker,
            part, got, chunk, chunk, part,
            V((NB, NA, Rb), bf16), V((NB, S - 1, OC, Rb), bf16),
            pltpu.SemaphoreType.DMA((5,)), pltpu.SemaphoreType.DMA((NB,)),
            pltpu.SemaphoreType.DMA((NB, 19)), pltpu.SemaphoreType.DMA((NB, 19)),
            pltpu.SemaphoreType.DMA((NB, 2, chips - 1)),
        ]
        half_out, turned = pl.pallas_call(
            functools.partial(kernel, (A, S, R, NA, NS, NI)),
            out_shape=(jax.ShapeDtypeStruct((R, NA), bf16), jax.ShapeDtypeStruct((OC, R), f32)),
            in_specs=[pl.BlockSpec(memory_space=pl.ANY)] * 5,
            out_specs=(pl.BlockSpec(memory_space=pl.ANY), pl.BlockSpec(memory_space=pltpu.VMEM)),
            scratch_shapes=scratch,
            compiler_params=pltpu.CompilerParams(
                collective_id=0, has_side_effects=True, vmem_limit_bytes=60 * 1024 * 1024),
        )(core_geno, noncore_geno, core_inv, snp_effects, noncore_scale.reshape(-1, 128))
        noncore_out, core_out = pl.pallas_call(
            widen,
            out_shape=(jax.ShapeDtypeStruct((R, NA), f32), jax.ShapeDtypeStruct((OC, R), f32)),
        )(half_out, turned)
        return noncore_out, core_out.T

    return jax.shard_map(
        local,
        mesh=mesh,
        in_specs=(P("anim", "snp"), P("anim", "snp"), P("anim", "snp"), P(None, "snp"), P("anim")),
        out_specs=(P(None, "anim"), P(None, ("anim", "snp"))),
        check_vma=False,
    )
```

```python
import functools

import jax
import jax.numpy as jnp
from jax import lax
from jax.experimental import pallas as pl
from jax.experimental.pallas import tpu as pltpu
from jax.sharding import PartitionSpec as P

NSNP = 49152
MESH = pl.DeviceIdType.MESH
BATCHES = 2
COL_SPLIT = 2
LAG = 1

f32 = jnp.float32
bf16 = jnp.bfloat16


def nt_dot(left, right):
    return lax.dot_general(
        left, right, (((1,), (1,)), ((), ())), preferred_element_type=f32
    )


def kernel(dims, core_hbm, noncore_hbm, inv_hbm, effects_hbm, scale_hbm,
           noncore_hbm_out, out_ref, *scratch):
    A, S, R, NA, NS, NI = dims
    NB, KC = BATCHES, COL_SPLIT
    Rb = R // NB
    KR = S // KC
    RC, W = Rb // KR, NA // KC
    chips = A // 2
    RA, H = Rb // chips, NS // 2
    OC = NA // S
    TN = min(256, W)
    TE = min(768, H)
    (core, noncore, inv, effects, scale,
     pa, np_, ra, cv, tb, vc,
     pd, rd, wc, wf,
     xe, xr, ye, yb, re_, ze, me,
     pf, rf, nc, nf,
     xg, xh, yg, yc, rg, zg, mg,
     ph, rh, cr, tr, vr,
     op, ri,
     insem, outsem, send, recv, agsem) = scratch
    a = lax.axis_index("anim")
    s = lax.axis_index("snp")
    chip = a // 2
    half = a % 2
    partner = a + 1 - 2 * half

    fold = S // 4
    away = (s // 2 + S // 2 - a // 2) % (S // 2)
    near = away // fold
    drop = near * (away - fold) + (1 - near) * (fold - 1 - away)
    turn_row = (((a // 4 + drop) % (A // 4)) * 2 + ((a // 2) % 2 + s % 2 + a % 2) % 2) * 2 + 1 - near
    rise = (a // 4 + A // 4 - s // 4) % (A // 4)
    reach = half * (fold - 1 - rise) + (1 - half) * (fold + rise)
    index = ((s // 2 + reach) % (S // 2)) * 2 + (s % 2 + (a // 2) % 2 + (s // 2) % 2) % 2

    def meet():
        pl.semaphore_wait(barrier, S + A - 1)

    def ring_step(j, n):
        return ((n - j) // 2) * (2 * (j % 2) - 1) % n

    rings, circles = S // 2, chips // 2
    snp_z, snp_x = s // 2, s % 2
    anim_y, anim_x = chip // 2, chip % 2
    flip = 1 - snp_x, snp_x
    side = 1 - anim_x, anim_x
    snp_peers = [lax.rem(snp_z + ring_step(i // 2, rings), rings) * 2 + flip[i % 2] for i in range(S - 1)]
    chip_peers = [lax.rem(anim_y + ring_step(i // 2, circles), circles) * 2 + side[i % 2] for i in range(chips - 1)]
    chip_backs = [lax.rem(anim_y + circles - ring_step(i // 2, circles), circles) * 2 + side[i % 2] for i in range(chips - 1)]
    anim_peers = [
        (lax.rem(anim_y + ring_step(i // 4, circles), circles) * 2 + side[i % 4 // 2]) * 2
        + (1 - half if i % 2 == 0 else half) for i in range(A - 1)]

    barrier = pltpu.get_barrier_semaphore()
    for k in snp_peers:
        pl.semaphore_signal(barrier, inc=1, device_id={"snp": k}, device_id_type=MESH)
    for k in anim_peers:
        pl.semaphore_signal(barrier, inc=1, device_id={"anim": k}, device_id_type=MESH)
    pl.semaphore_signal(barrier, inc=1, device_id={"anim": s, "snp": index}, device_id_type=MESH)

    loads = [(effects_hbm, effects), (core_hbm, core), (noncore_hbm, noncore),
             (inv_hbm, inv), (scale_hbm, scale)]
    copies = [pltpu.make_async_copy(x, y, insem.at[i]) for i, (x, y) in enumerate(loads)]
    for c in copies:
        c.start()

    def rows(k):
        return pl.ds(pl.multiple_of((k // KC) * RC, RC), RC)

    def cols(k):
        return pl.ds(pl.multiple_of((k % KC) * W, W), W)

    def wait_bytes(ref, sem):
        pltpu.make_async_copy(ref, ref, sem).wait()

    ends = []

    def send_part(b, phase, part, got, which):
        for r in which:
            k = snp_peers[r]
            pltpu.make_async_remote_copy(
                part.at[b, rows(k), cols(k)], got.at[b, r],
                send.at[b, phase], recv.at[b, phase],
                device_id={"snp": k}, device_id_type=MESH).start()

    def rs_snp(b, phase, part, got):
        send_part(b, phase, part, got, range(S - 1))
        ends.append((got.at[b], b, phase))

    def tiles_rs_snp(b, phase, part, got, body):
        early = -(-W // TN) * TN
        late = NA - early
        body(pl.ds(pl.multiple_of((1 - snp_x) * late, TN), early))
        send_part(b, phase, part, got, range(0, S - 1, 2))
        body(pl.ds(pl.multiple_of(snp_x * early, TN), late))
        send_part(b, phase, part, got, range(1, S - 1, 2))
        ends.append((got.at[b], b, phase))

    def sum_snp(b, phase, part, got):
        wait_bytes(got.at[b], recv.at[b, phase])
        total = part[b, rows(s), cols(s)].astype(f32)
        for r in range(S - 1):
            total = total + got[b, r].astype(f32)
        return total

    def ag_snp(b, phase, chunk, whole, proxy):
        for r in range(S - 1):
            pltpu.make_async_remote_copy(
                chunk.at[b], whole.at[b, rows(s), cols(s)],
                send.at[b, phase], recv.at[b, phase],
                device_id={"snp": snp_peers[r]}, device_id_type=MESH).start()
        whole[b, rows(s), cols(s)] = chunk[b]
        ends.append((proxy.at[b], b, phase))

    def turn(b, phase, chunk, landed):
        pltpu.make_async_remote_copy(
            chunk.at[b], landed.at[b], send.at[b, phase], recv.at[b, phase],
            device_id={"anim": turn_row, "snp": a}, device_id_type=MESH).start()
        ends.append((landed.at[b], b, phase))

    def ag_anim(b, turned, phase, landed, whole, proxy):
        wait_bytes(landed.at[b], recv.at[b, turned])

        for r in range(A - 1):
            pltpu.make_async_remote_copy(
                landed.at[b], whole.at[b, rows(index), cols(index)],
                send.at[b, phase], recv.at[b, phase],
                device_id={"anim": anim_peers[r]}, device_id_type=MESH).start()
        whole[b, rows(index), cols(index)] = landed[b]
        ends.append((proxy.at[b], b, phase))

    def marker_product(b, phase, left, geno, out_half, in_half, own):
        lhs = left[b]

        def other(t, _):
            at = pl.ds(pl.multiple_of((1 - half) * H + t * TE, TE), TE)
            to = pl.ds(pl.multiple_of(t * TE, TE), TE)
            out_half[b, :, to] = jnp.dot(lhs, geno[:, at], preferred_element_type=f32).astype(bf16)
            pltpu.make_async_remote_copy(
                out_half.at[b, :, to], in_half.at[b, :, to],
                send.at[b, phase], recv.at[b, phase],
                device_id={"anim": partner}, device_id_type=MESH).start()
            return 0
        lax.fori_loop(0, H // TE, other, 0)

        own[b] = jnp.dot(lhs, geno[:, half_cols(half)], preferred_element_type=f32)
        ends.append((in_half.at[b], b, phase))

    def chip_rows(c):
        return pl.ds(pl.multiple_of(c * RA, RA), RA)

    def rs_chips(b, crossed, phase, in_half, own, both, got):
        wait_bytes(in_half.at[b], recv.at[b, crossed])

        for r in range(chips - 1):
            c = chip_peers[r]
            at = chip_rows(c)
            both[b, at, :] = (own[b, at, :] + in_half[b, at, :].astype(f32)).astype(bf16)
            pltpu.make_async_remote_copy(
                both.at[b, at, :], got.at[b, r],
                send.at[b, phase], recv.at[b, phase],
                device_id={"anim": 2 * c + half}, device_id_type=MESH).start()
        ends.append((got.at[b], b, phase))

    def half_cols(h):
        return pl.ds(pl.multiple_of(h * H, H), H)

    def ag_chips(b, summed, phase, cross, slot, in_half, own, got, chunk, whole):
        at = chip_rows(chip)
        total = own[b, at, :] + in_half[b, at, :].astype(f32)
        wait_bytes(got.at[b], recv.at[b, summed])
        for r in range(chips - 1):
            total = total + got[b, r].astype(f32)
        chunk[b] = (total / NSNP).astype(bf16)
        spot = whole.at[b, at, half_cols(half)]

        for r in range(chips - 1):
            pltpu.make_async_remote_copy(
                chunk.at[b], spot, send.at[b, phase], agsem.at[b, slot, r],
                device_id={"anim": 2 * chip_peers[r] + half}, device_id_type=MESH).start()
        pltpu.make_async_remote_copy(
            chunk.at[b], spot, send.at[b, cross], recv.at[b, cross],
            device_id={"anim": partner}, device_id_type=MESH).start()
        whole[b, at, half_cols(half)] = chunk[b]
        ends.append((got.at[b], b, phase))
        ends.append((in_half.at[b], b, cross))

    def relay(b, cross, slot, whole):
        for r in range(chips - 1):
            spot = whole.at[b, chip_rows(chip_backs[r]), half_cols(half)]
            wait_bytes(spot, agsem.at[b, slot, r])
            pltpu.make_async_remote_copy(
                spot, spot, send.at[b, cross], recv.at[b, cross],
                device_id={"anim": partner}, device_id_type=MESH).start()

    def rep_rows(b):
        return pl.ds(b * Rb, Rb)

    everywhere = pl.ds(0, NA)

    def s0(b):
        if b == 0:
            copies[0].wait()
            copies[1].wait()

        def body(at):
            pa[b, :, at] = nt_dot(effects[rep_rows(b), :], core[at, :]).astype(bf16)
        body(everywhere)

    def s0a(b):
        if b == 0:
            meet()
        rs_snp(b, 0, pa, ra)

    def s0b(b):
        if b == 0:
            copies[2].wait()

        def body(at):
            np_[b, :, at] = nt_dot(effects[rep_rows(b), :], noncore[at, :])
        body(everywhere)

    def s1(b):
        cv[b] = sum_snp(b, 0, pa, ra).astype(bf16)
        turn(b, 1, cv, tb)

    def s2(b):
        ag_anim(b, 1, 2, tb, vc, ra)

    def s3(b):
        if b == 0:
            copies[3].wait()
        wait_bytes(ra.at[b], recv.at[b, 2])

        def body(at):
            pd[b, :, at] = nt_dot(vc[b], inv[at, :]).astype(bf16)
        tiles_rs_snp(b, 3, pd, rd, body)

    def s4(b):
        wc[b] = sum_snp(b, 3, pd, rd).astype(bf16)
        ag_snp(b, 4, wc, wf, rd)

    def s5(b):
        wait_bytes(rd.at[b], recv.at[b, 4])
        marker_product(b, 5, wf, core, xe, xr, ye)

    def s6(b):
        rs_chips(b, 5, 6, xr, ye, yb, re_)

    def s7(b):
        ag_chips(b, 6, 7, 8, 0, xr, ye, re_, ze, me)

    def s8(b):
        relay(b, 8, 0, me)

        def body(at):
            np_[b, :, at] = np_[b, :, at] - nt_dot(me[b, :, half_cols(half)], noncore[at, half_cols(half)])
        body(everywhere)

    def s9(b):
        wait_bytes(xr.at[b], recv.at[b, 8])

        def body(at):
            pf[b, :, at] = (np_[b, :, at] - nt_dot(
                me[b, :, half_cols(1 - half)], noncore[at, half_cols(1 - half)])).astype(bf16)
        tiles_rs_snp(b, 9, pf, rf, body)

    def s10(b):
        if b == 0:
            copies[4].wait()
        first = (s % KC) * (W // 128)
        line = jnp.concatenate([scale[pl.ds(first + q, 1), :] for q in range(W // 128)], axis=1)
        nc[b] = (line * sum_snp(b, 9, pf, rf)).astype(bf16)
        ag_snp(b, 10, nc, nf, rf)

    def s11(b):
        wait_bytes(rf.at[b], recv.at[b, 10])
        pltpu.make_async_copy(nf.at[b], noncore_hbm_out.at[rep_rows(b), :], outsem.at[b]).start()
        marker_product(b, 11, nf, noncore, xg, xh, yg)

    def s12(b):
        rs_chips(b, 11, 12, xh, yg, yc, rg)

    def s13(b):
        ag_chips(b, 12, 13, 14, 1, xh, yg, rg, zg, mg)

    def s14(b):
        relay(b, 14, 1, mg)

        def body(at):
            np_[b, :, at] = nt_dot(mg[b, :, half_cols(half)], core[at, half_cols(half)])
        body(everywhere)

    def s15(b):
        wait_bytes(xh.at[b], recv.at[b, 14])

        def body(at):
            ph[b, :, at] = (np_[b, :, at] + nt_dot(
                mg[b, :, half_cols(1 - half)], core[at, half_cols(1 - half)])).astype(bf16)
        tiles_rs_snp(b, 15, ph, rh, body)

    def s16(b):
        cr[b] = (cv[b].astype(f32) - sum_snp(b, 15, ph, rh)).astype(bf16)
        turn(b, 16, cr, tr)

    def s17(b):
        ag_anim(b, 16, 17, tr, vr, rh)

    def s18(b):
        wait_bytes(rh.at[b], recv.at[b, 17])

        op[b] = nt_dot(inv[...], vr[b]).astype(bf16)

        for r in range(S - 1):
            k = snp_peers[r]
            pltpu.make_async_remote_copy(
                op.at[b, pl.ds(pl.multiple_of(k * OC, OC), OC), :], ri.at[b, r],
                send.at[b, 18], recv.at[b, 18],
                device_id={"snp": k}, device_id_type=MESH).start()
        ends.append((ri.at[b], b, 18))

    def s19(b):
        wait_bytes(ri.at[b], recv.at[b, 18])
        total = op[b, pl.ds(pl.multiple_of(s * OC, OC), OC), :].astype(f32)
        for r in range(S - 1):
            total = total + ri[b, r].astype(f32)
        out_ref[:, b * Rb:(b + 1) * Rb] = total

    stages = [s0, s0a, s0b, s1, s2, s3, s4, s5, s6, s7, s8, s9, s10, s11, s12, s13,
              s14, s15, s16, s17, s18, s19]
    order = sorted((i + LAG * b, b, i) for i in range(len(stages)) for b in range(NB))
    order[-3], order[-2] = order[-2], order[-3]
    for _, b, i in order:
        stages[i](b)

    for ref, b, phase in ends:
        wait_bytes(ref, send.at[b, phase])
    for b in range(NB):
        wait_bytes(nf.at[b], outsem.at[b])


def widen(half_ref, turned_ref, noncore_ref, core_ref):
    noncore_ref[...] = half_ref[...].astype(f32)
    core_ref[...] = turned_ref[...]


def solution(mesh):
    A, S = mesh.shape["anim"], mesh.shape["snp"]

    def local(core_geno, noncore_geno, core_inv, snp_effects, noncore_scale):
        R = snp_effects.shape[0]
        NA, NS = core_geno.shape
        NI = core_inv.shape[1]
        NB, KC = BATCHES, COL_SPLIT
        Rb = R // NB
        KR = S // KC
        RC, W = Rb // KR, NA // KC
        chips = A // 2
        RA, H = Rb // chips, NS // 2
        OC = NA // S
        V = pltpu.VMEM
        chunk = V((NB, RC, W), bf16)
        part = V((NB, Rb, NA), bf16)
        got = V((NB, S - 1, RC, W), bf16)
        halfb = V((NB, Rb, H), bf16)
        marker = [halfb, halfb, V((NB, Rb, H), f32), halfb,
                  V((NB, chips - 1, RA, H), bf16), V((NB, RA, H), bf16), V((NB, Rb, NS), bf16)]
        scratch = [
            V((NA, NS), bf16), V((NA, NS), bf16), V((NA, NI), bf16), V((R, NS), bf16), V((NA // 128, 128), f32),
            part, V((NB, Rb, NA), f32), got, chunk, chunk, part,
            part, got, chunk, part,
            *marker,
            part, got, chunk, part,
            *marker,
            part, got, chunk, chunk, part,
            V((NB, NA, Rb), bf16), V((NB, S - 1, OC, Rb), bf16),
            pltpu.SemaphoreType.DMA((5,)), pltpu.SemaphoreType.DMA((NB,)),
            pltpu.SemaphoreType.DMA((NB, 19)), pltpu.SemaphoreType.DMA((NB, 19)),
            pltpu.SemaphoreType.DMA((NB, 2, chips - 1)),
        ]
        half_out, turned = pl.pallas_call(
            functools.partial(kernel, (A, S, R, NA, NS, NI)),
            out_shape=(jax.ShapeDtypeStruct((R, NA), bf16), jax.ShapeDtypeStruct((OC, R), f32)),
            in_specs=[pl.BlockSpec(memory_space=pl.ANY)] * 5,
            out_specs=(pl.BlockSpec(memory_space=pl.ANY), pl.BlockSpec(memory_space=pltpu.VMEM)),
            scratch_shapes=scratch,
            compiler_params=pltpu.CompilerParams(
                collective_id=0, has_side_effects=True, vmem_limit_bytes=60 * 1024 * 1024),
        )(core_geno, noncore_geno, core_inv, snp_effects, noncore_scale.reshape(-1, 128))
        noncore_out, core_out = pl.pallas_call(
            widen,
            grid=(2,),
            out_shape=(jax.ShapeDtypeStruct((R, NA), f32), jax.ShapeDtypeStruct((OC, R), f32)),
            in_specs=[pl.BlockSpec((R // 2, NA), lambda g: (g, 0)), pl.BlockSpec((OC, R // 2), lambda g: (0, g))],
            out_specs=(pl.BlockSpec((R // 2, NA), lambda g: (g, 0)), pl.BlockSpec((OC, R // 2), lambda g: (0, g))),
        )(half_out, turned)
        return noncore_out, core_out.T

    return jax.shard_map(
        local,
        mesh=mesh,
        in_specs=(P("anim", "snp"), P("anim", "snp"), P("anim", "snp"), P(None, "snp"), P("anim")),
        out_specs=(P(None, "anim"), P(None, ("anim", "snp"))),
        check_vma=False,
    )
```
